32 devices in a mesh: dp: 2 (over x), expert: 16 (over z, y, core).
Axes of the slice: x: 2, y: 2, z: 4, core: 2. Of those that a mesh axis runs over, the one named last changes fastest.
Arguments:
- hidden: bfloat16 [4096, 1024], P(('dp', 'expert')), may hold values from -6 to 6
- grad_out: bfloat16 [4096, 1024], P(('dp', 'expert')), may hold values from -48 to 48
- router_weight: float32 [1024, 16], replicated, may hold values from -0.1875 to 0.1875
- expert_ids: int32 [4096, 6], P(('dp', 'expert')), may hold values from 0 to 15, all different within a row; in each aligned block of 64 rows (0 to 63, 64 to 127, ...) at most 25 rows name the same one
- pre_gate: bfloat16 [2, 16, 800, 704], P('dp', 'expert'), may hold values from -6 to 6
- pre_up: bfloat16 [2, 16, 800, 704], P('dp', 'expert'), may hold values from -6 to 6
- w_gate: bfloat16 [16, 1024, 704], P('expert'), may hold values from -0.1875 to 0.1875
- w_up: bfloat16 [16, 1024, 704], P('expert'), may hold values from -0.1875 to 0.1875
- w_down: bfloat16 [16, 704, 1024], P('expert'), may hold values from -0.21875 to 0.21875
Outputs:
- grad_x: bfloat16 [4096, 1024], P(('dp', 'expert'))
- router_update: float32 [1024, 16], P('dp', 'expert')
The draws below stay inside these ranges and needn't reach their ends.
Inputs may be any that keep to these rules, and one draw needn't show every extreme that they name: `expert_ids`: each row names 6 different experts; in each aligned block of 64 rows no expert is named by more than 25 rows.
All inputs are finite; a program needn't handle non-finite values.
Results may differ from the reference program's by a relative error of at most 0.006.
Values may be sent and summed in bfloat16 or wider, within the bound.
No kernel may reach another device: no remote copies, remote signals or barrier semaphores. Data moves between devices by JAX's collectives and lax.ppermute only.
A program may use at most 64 MiB of HBM per device.

```python
import math
import jax
import jax.numpy as jnp
import numpy as np
from jax import lax

D = 1024
FF = 704
TOK_DEV = 128
BLK = 64
EXPERTS = 16
TOP = 6
CAP = 25
TOKENS = 4096
N_DP = 2
N_EXPERT = 16


def levels(key, shape, cuts, smallest, top_value):
    level = 1.0
    for axis_at, shards_of in cuts:
        heights = jax.random.uniform(jax.random.fold_in(jax.random.fold_in(key, 6), axis_at), (shards_of,), jnp.float32, smallest / len(cuts), top_value / len(cuts))
        level = level * jnp.repeat(jnp.exp(heights), shape[axis_at] // shards_of).reshape((-1,) + (1,) * (len(shape) - 1 - axis_at))
    return level


def routed_block(key, own, number, rows, count, top, most, lean):
    ranking = jax.random.permutation(key, count)
    heavy_load, usual = shares(count, rows * top, most, lean, True), shares(count, rows * top, most, lean, False)
    places = jnp.arange(count)

    def named(sizes, turn):
        used = int((sizes > 0).sum())
        fixed = max(1, used // 4)
        moved = fixed + (places - fixed + turn * (used - fixed)) % max(1, count - fixed)
        return jnp.zeros((count,), jnp.int32).at[ranking[jnp.where(places < fixed, places, moved)]].set(jnp.asarray(sizes, jnp.int32))

    sizes = jnp.where(number % 4 == 0, named(heavy_load, number // 4), named(usual, number - number // 4 - 1))
    mixed = jax.random.permutation(jax.random.fold_in(own, 3), count)
    donor, taker = mixed[0:count // 2 * 2:2], mixed[1:count // 2 * 2:2]
    margin = jnp.minimum(sizes[donor] - 1, most - sizes[taker]) // 2
    margin = jnp.where((donor == ranking[0]) | (taker == ranking[0]) | (sizes[taker] == 0), 0, jnp.maximum(margin, 0))
    moved = jax.random.randint(jax.random.fold_in(own, 4), (count // 2,), 0, 1 << 20) % (margin + 1)
    sizes = sizes.at[donor].add(-moved).at[taker].add(moved)
    labels = jnp.searchsorted(jnp.cumsum(sizes), jnp.arange(rows * top), side="right").astype(jnp.int32)
    table = labels.reshape(top, rows).T
    table = table[jax.random.permutation(jax.random.fold_in(own, 1), rows)]
    turn = jax.random.randint(jax.random.fold_in(own, 2), (rows, 1), 0, top)
    return jnp.take_along_axis(table, (jnp.arange(top)[None, :] + turn) % top, axis=1)


def shares(count, total, reach, slope, full):
    portions = [(1 << 20) // math.isqrt(grade ** slope) + 1 for grade in range(1, count + 1)]
    largest = reach if full else min(reach, max(-(-total // count), total * portions[0] // sum(portions)))
    least = 1 if total - largest >= count - 1 else 0
    given, rest = [largest] + [least] * (count - 1), total - largest - least * (count - 1)
    while rest > 0:
        movable = [i for i in range(1, count) if given[i] < largest] or [i for i in range(1, count) if given[i] < reach]
        pool, left = sum([portions[i] for i in movable]), rest
        for i in movable:
            extra = min(reach - given[i], max(1, left * portions[i] // pool), rest)
            given[i] = given[i] + extra
            rest = rest - extra
    return np.array(given)


def normal_values(own_key, dims, scale, bound, cuts=(), kind=jnp.bfloat16):
    factor_of = levels(own_key, dims, cuts, -0.22, 0.18) if cuts else 1.0
    array = jax.random.normal(own_key, dims, jnp.float32) * scale * factor_of
    return jnp.minimum(jnp.maximum(array, -bound), bound).astype(kind)


def setup_inputs(seed: int = 0) -> dict:
    seeds = jax.random.split(jax.random.key(seed), 10)
    hidden = normal_values(seeds[0], (TOKENS, D), 1.0, 6.0, ((0, 32),))
    grad_out = normal_values(seeds[1], (TOKENS, D), 8.0, 48.0, ((0, 32),))
    router_weight = normal_values(seeds[2], (D, EXPERTS), D ** -0.5, 0.1875, (), jnp.float32)
    expert_ids_keys = jax.random.split(jax.random.fold_in(seeds[3], 1), TOKENS // BLK)
    expert_ids_turns = jax.random.permutation(jax.random.fold_in(seeds[3], 3), TOKENS // BLK)
    expert_ids = jax.vmap(lambda own, number: routed_block(jax.random.fold_in(seeds[3], 2), own, number, BLK, EXPERTS, TOP, CAP, 2))(expert_ids_keys, expert_ids_turns).reshape((TOKENS, TOP))
    pre_gate = normal_values(seeds[4], (N_DP, EXPERTS, (TOK_DEV // BLK) * N_EXPERT * CAP, FF), 1.0, 6.0, ((0, 2), (1, 16)))
    pre_up = normal_values(seeds[5], (N_DP, EXPERTS, (TOK_DEV // BLK) * N_EXPERT * CAP, FF), 1.0, 6.0, ((0, 2), (1, 16)))
    w_gate = normal_values(seeds[6], (EXPERTS, D, FF), D ** -0.5, 0.1875, ((0, 16),))
    w_up = normal_values(seeds[7], (EXPERTS, D, FF), D ** -0.5, 0.1875, ((0, 16),))
    w_down = normal_values(seeds[8], (EXPERTS, FF, D), FF ** -0.5, 0.21875, ((0, 16),))
    return {"hidden": hidden, "grad_out": grad_out, "router_weight": router_weight, "expert_ids": expert_ids, "pre_gate": pre_gate, "pre_up": pre_up, "w_gate": w_gate, "w_up": w_up, "w_down": w_down}


PRECISE = lax.Precision.HIGHEST

def contract_last(left, right):
    return lax.dot_general(left, right, (((1,), (1,)), ((), ())), preferred_element_type=jnp.float32)

def slot_places(group_ids, block_rows, experts, capacity):
    tokens, top = group_ids.shape
    grouped = group_ids.reshape(tokens // block_rows, block_rows * top).astype(jnp.int32)
    hit_marks = (grouped[..., None] == jnp.arange(experts, dtype=jnp.int32)).astype(jnp.int32)
    earlier = jnp.cumsum(hit_marks, axis=1) - hit_marks
    slot_index = lax.optimization_barrier(jnp.sum(earlier * hit_marks, axis=-1)).astype(jnp.int32)
    flat_place = (grouped * capacity + slot_index).astype(jnp.int32)
    places = (flat_place[..., None] == jnp.arange(experts * capacity, dtype=jnp.int32)).astype(jnp.float32)
    return places.reshape(tokens // block_rows, block_rows, top, experts, capacity)

def expert_backward(sent_rows, gate_values, saved_gate, saved_up, w_gate, w_up, w_down):
    model_width = sent_rows.shape[-1]
    flat_rows = sent_rows.reshape(-1, model_width)
    dh_raw = contract_last(flat_rows, w_down)
    pre_first = saved_gate.reshape(-1, saved_gate.shape[-1]).astype(jnp.float32)
    pre_second = saved_up.reshape(-1, saved_up.shape[-1]).astype(jnp.float32)
    sigmoid_value = jax.nn.sigmoid(pre_first)
    active = pre_first * sigmoid_value
    slope_value = sigmoid_value * (1.0 + pre_first * (1.0 - sigmoid_value))
    gate_grad = lax.optimization_barrier(jnp.sum(dh_raw * active * pre_second, axis=-1))
    dh_scaled = gate_values.reshape(-1, 1).astype(jnp.float32) * dh_raw
    d_first = (dh_scaled * pre_second * slope_value).astype(jnp.bfloat16)
    d_second = (dh_scaled * active).astype(jnp.bfloat16)
    back_rows = contract_last(d_first, w_gate) + contract_last(d_second, w_up)
    return (back_rows.astype(jnp.bfloat16).reshape(sent_rows.shape), gate_grad.astype(jnp.bfloat16).reshape(sent_rows.shape[:-1]))

def reference(hidden, grad_out, router_weight, expert_ids, pre_gate, pre_up, w_gate, w_up, w_down):
    block_count = TOK_DEV // BLK
    model_width = hidden.shape[1]
    group_tokens = N_EXPERT * TOK_DEV
    logits = jnp.dot(hidden.astype(jnp.float32), router_weight, precision=PRECISE)
    exponent = jnp.exp(logits)
    probability = exponent / lax.optimization_barrier(jnp.sum(exponent, axis=-1, keepdims=True))
    picked = (expert_ids[..., None] == jnp.arange(EXPERTS, dtype=jnp.int32)).astype(jnp.float32)
    gate_values = lax.optimization_barrier(jnp.sum(picked * probability[:, None, :], axis=-1))

    def one_group(pieces):
        group_ids, cotangent, group_gates, saved_gate, saved_up = pieces
        places = slot_places(group_ids, BLK, EXPERTS, CAP).reshape(N_EXPERT, block_count, BLK, TOP, EXPERTS, CAP)
        chosen = lax.optimization_barrier(jnp.sum(places, axis=3))
        dense_rows = cotangent.reshape(N_EXPERT, block_count, BLK, model_width).astype(jnp.float32)
        sent_rows = jnp.einsum('snbec,snbd->enscd', chosen, dense_rows, precision=PRECISE).astype(jnp.bfloat16)
        sent_gate = jnp.einsum('snbkec,snbk->ensc', places, group_gates.reshape(N_EXPERT, block_count, BLK, TOP), precision=PRECISE).astype(jnp.bfloat16)
        saved_first = saved_gate.reshape(EXPERTS, block_count, N_EXPERT, CAP, saved_gate.shape[-1])
        saved_second = saved_up.reshape(EXPERTS, block_count, N_EXPERT, CAP, saved_up.shape[-1])

        def one_expert(items):
            return expert_backward(*items)
        back_rows, gate_grad = lax.map(one_expert, (sent_rows, sent_gate, saved_first, saved_second, w_gate, w_up, w_down))
        moe_part = jnp.einsum('snbec,enscd->snbd', chosen, back_rows.astype(jnp.float32), precision=PRECISE)
        gate_part = jnp.einsum('snbkec,ensc->snbk', places, gate_grad.astype(jnp.float32), precision=PRECISE)
        return (moe_part.reshape(group_tokens, model_width), gate_part.reshape(group_tokens, TOP))
    moe_grad, gate_grad = lax.map(one_group, (expert_ids.reshape(N_DP, group_tokens, TOP), grad_out.reshape(N_DP, group_tokens, model_width), gate_values.reshape(N_DP, group_tokens, TOP), pre_gate, pre_up))
    moe_grad = moe_grad.reshape(TOKENS, model_width)
    gate_grad = gate_grad.reshape(TOKENS, TOP)
    prob_grad = lax.optimization_barrier(jnp.sum(picked * gate_grad[..., None], axis=1))
    logit_grad = probability * (prob_grad - lax.optimization_barrier(jnp.sum(probability * prob_grad, axis=-1, keepdims=True)))
    grad_x = (moe_grad + jnp.dot(logit_grad, router_weight.T, precision=PRECISE)).astype(jnp.bfloat16)
    router_term = jnp.dot(hidden.astype(jnp.float32).T, logit_grad, precision=PRECISE)
    square_total = jnp.sum(router_term * router_term)
    factor = jnp.minimum(1.0, jnp.sqrt(model_width * EXPERTS / (square_total + 1e-06)))
    return (grad_x, router_term * factor)
```

```python
import jax
import jax.numpy as jnp
from jax import lax
from jax.sharding import PartitionSpec as P

BLK = 64


PRECISE = lax.Precision.HIGHEST


def contract_last(left, right):
    return lax.dot_general(
        left, right, (((1,), (1,)), ((), ())), preferred_element_type=jnp.float32
    )


def slot_places(group_ids, block_rows, experts, capacity):
    tokens, top = group_ids.shape
    grouped = group_ids.reshape(tokens // block_rows, block_rows * top)
    hit_marks = (grouped[..., None] == jnp.arange(experts, dtype=jnp.int32)).astype(jnp.int32)
    earlier = jnp.cumsum(hit_marks, axis=1) - hit_marks
    slot_index = jnp.sum(earlier * hit_marks, axis=-1)
    flat_place = grouped * capacity + slot_index
    places = (flat_place[..., None] == jnp.arange(experts * capacity, dtype=jnp.int32)).astype(
        jnp.float32
    )
    return places.reshape(tokens // block_rows, block_rows, top, experts, capacity)


def expert_backward(sent_rows, gate_values, saved_gate, saved_up, w_gate, w_up, w_down):
    model_width = sent_rows.shape[-1]
    flat_rows = sent_rows.reshape(-1, model_width)
    dh_raw = contract_last(flat_rows, w_down)
    pre_first = saved_gate.reshape(-1, saved_gate.shape[-1]).astype(jnp.float32)
    pre_second = saved_up.reshape(-1, saved_up.shape[-1]).astype(jnp.float32)
    sigmoid_value = jax.nn.sigmoid(pre_first)
    active = pre_first * sigmoid_value
    slope_value = sigmoid_value * (1.0 + pre_first * (1.0 - sigmoid_value))
    gate_grad = jnp.sum(dh_raw * active * pre_second, axis=-1)
    dh_scaled = gate_values.reshape(-1, 1).astype(jnp.float32) * dh_raw
    d_first = (dh_scaled * pre_second * slope_value).astype(jnp.bfloat16)
    d_second = (dh_scaled * active).astype(jnp.bfloat16)
    back_rows = contract_last(d_first, w_gate) + contract_last(d_second, w_up)
    return (
        back_rows.astype(jnp.bfloat16).reshape(sent_rows.shape),
        gate_grad.astype(jnp.bfloat16).reshape(sent_rows.shape[:-1]),
    )


def local(hidden, grad_out, router_weight, expert_ids, pre_gate, pre_up, w_gate, w_up, w_down):
    tokens, model_width = hidden.shape
    experts = router_weight.shape[1]
    block_count = tokens // BLK
    senders = lax.axis_size("expert")
    capacity = pre_gate.shape[2] // (block_count * senders)
    places = slot_places(expert_ids, BLK, experts, capacity)
    chosen = jnp.sum(places, axis=2)
    logits = jnp.dot(hidden.astype(jnp.float32), router_weight, precision=PRECISE)
    exponent = jnp.exp(logits)
    probability = exponent / jnp.sum(exponent, axis=-1, keepdims=True)
    picked = (expert_ids[..., None] == jnp.arange(experts, dtype=jnp.int32)).astype(jnp.float32)
    gate_values = jnp.sum(picked * probability[:, None, :], axis=-1)
    sent_rows = jnp.einsum(
        "nbec,nbd->necd",
        chosen.astype(jnp.bfloat16),
        grad_out.reshape(block_count, BLK, model_width),
        preferred_element_type=jnp.float32,
    ).astype(jnp.bfloat16)
    sent_gate = jnp.einsum(
        "nbkec,nbk->nec", places, gate_values.reshape(block_count, BLK, -1), precision=PRECISE
    ).astype(jnp.bfloat16)
    saved_first = pre_gate.reshape(block_count, senders, capacity, pre_gate.shape[-1])
    saved_second = pre_up.reshape(block_count, senders, capacity, pre_up.shape[-1])
    gate_matrix = w_gate[0]
    up_matrix = w_up[0]
    down_matrix = w_down[0]
    arrived, arrived_gate = (
        lax.all_to_all(sent_rows, "expert", split_axis=1, concat_axis=1, tiled=True),
        lax.all_to_all(sent_gate, "expert", split_axis=1, concat_axis=1, tiled=True),
    )
    back_rows, gate_grad = expert_backward(
        arrived, arrived_gate, saved_first, saved_second, gate_matrix, up_matrix, down_matrix
    )
    returned, returned_gate = (
        lax.all_to_all(back_rows, "expert", split_axis=1, concat_axis=1, tiled=True),
        lax.all_to_all(gate_grad, "expert", split_axis=1, concat_axis=1, tiled=True),
    )
    moe_grad = jnp.einsum(
        "nbec,necd->nbd", chosen.astype(jnp.bfloat16), returned, preferred_element_type=jnp.float32
    ).reshape(tokens, model_width)
    token_gate_grad = jnp.einsum(
        "nbkec,nec->nbk", places, returned_gate.astype(jnp.float32), precision=PRECISE
    ).reshape(tokens, -1)
    prob_grad = jnp.sum(picked * token_gate_grad[..., None], axis=1)
    logit_grad = probability * (
        prob_grad - jnp.sum(probability * prob_grad, axis=-1, keepdims=True)
    )
    grad_x = (moe_grad + jnp.dot(logit_grad, router_weight.T, precision=PRECISE)).astype(
        jnp.bfloat16
    )
    router_term = jnp.dot(hidden.astype(jnp.float32).T, logit_grad, precision=PRECISE)
    groups, axes = lax.axis_size("dp"), ("dp", "expert")
    pieces = router_term.reshape(groups, model_width // groups, senders, experts // senders)
    pieces = pieces.transpose(0, 2, 3, 1).reshape(groups * senders, -1)
    router_share = jnp.sum(lax.all_to_all(pieces, axes, 0, 0, tiled=True), axis=0)
    square = jnp.broadcast_to(jnp.sum(router_share * router_share), (groups * senders, 128))
    square_total = jnp.sum(lax.all_to_all(square, axes, 0, 0, tiled=True)[:, 0])
    router_share = router_share.reshape(experts // senders, -1).T
    factor = jnp.minimum(1.0, jnp.sqrt(model_width * experts / (square_total + 1e-06)))
    return (grad_x, router_share * factor)


def solution(mesh):
    placed = (
        P(("dp", "expert"), None),
        P(("dp", "expert"), None),
        P(),
        P(("dp", "expert"), None),
        P("dp", "expert", None, None),
        P("dp", "expert", None, None),
        P("expert", None, None),
        P("expert", None, None),
        P("expert", None, None),
    )
    return jax.shard_map(
        local,
        mesh=mesh,
        in_specs=placed,
        out_specs=(P(("dp", "expert"), None), P("dp", "expert")),
        check_vma=False,
    )
```

```python
import functools

import jax
import jax.numpy as jnp
from jax import lax
from jax.experimental import pallas as pl
from jax.experimental.pallas import tpu as pltpu
from jax.sharding import PartitionSpec as P


BLK = 64
LANES = 128
PLANES = 4
CORES = 2
ROWS = 8
ROOM = 6


NT = (((1,), (1,)), ((), ()))
TN = (((0,), (0,)), ((), ()))
NN = (((1,), (0,)), ((), ()))


def dot(left, right, dims):
    return lax.dot_general(left, right, dims, preferred_element_type=jnp.float32)


def three_parts(value):
    first = value.astype(jnp.bfloat16)
    rest = value - first.astype(jnp.float32)
    second = rest.astype(jnp.bfloat16)
    return first, second, (rest - second.astype(jnp.float32)).astype(jnp.bfloat16)


def call(kernel, out_shape, *operands, spaces="", outs="", scratch=()):
    kinds = {
        "v": pl.BlockSpec(memory_space=pltpu.VMEM),
        "b": pl.BlockSpec(),
        "s": pl.BlockSpec(memory_space=pltpu.SMEM),
        "h": pl.BlockSpec(memory_space=pltpu.HBM),
    }
    spaces = spaces.ljust(len(operands), "v")
    operands = [
        pltpu.with_memory_space_constraint(a, pltpu.HBM) if c == "h" else a
        for a, c in zip(operands, spaces)
    ]
    return pl.pallas_call(
        kernel,
        out_shape=out_shape,
        in_specs=[kinds[c] for c in spaces],
        out_specs=[kinds[c] for c in outs.ljust(len(out_shape), "v")],
        scratch_shapes=scratch,
        compiler_params=pltpu.CompilerParams(vmem_limit_bytes=ROOM << 20),
    )(*operands)


def fetch_kernel(*refs):
    count = (len(refs) - 1) // 2
    copies = [
        pltpu.make_async_copy(refs[i], refs[count + i], refs[-1].at[i]) for i in range(count)
    ]
    for copy in copies:
        copy.start()
    for copy in copies:
        copy.wait()


def front_kernel(*refs):
    sent_ref, prob_ref, me_ref, hidden_ref, router_ref, ids_ref, sems = refs[5:]
    me_ref[0] = refs[4][0]
    experts, tokens = prob_ref.shape
    targets = (hidden_ref, router_ref, ids_ref, sent_ref.at[pl.ds(0, tokens)])
    copies = [pltpu.make_async_copy(refs[i], targets[i], sems.at[i]) for i in range(4)]
    for copy in copies:
        copy.start()
    for copy in copies:
        copy.wait()
    hidden = hidden_ref[...]
    logits = sum(dot(part, hidden, NT) for part in three_parts(router_ref[...]))
    exponent = jnp.exp(logits)
    prob = exponent / jnp.sum(exponent, axis=0, keepdims=True)
    prob_ref[...] = prob
    number = lax.broadcasted_iota(jnp.int32, (experts, tokens), 0)
    ids = ids_ref[...]
    named = number == ids[0:1, :]
    for k in range(1, ids.shape[0]):
        named = named | (number == ids[k : k + 1, :])
    row = lax.broadcasted_iota(jnp.int32, (tokens, tokens), 0)
    column = lax.broadcasted_iota(jnp.int32, (tokens, tokens), 1)
    before = (row < column) & (row // BLK == column // BLK)
    rank = dot(named.astype(jnp.bfloat16), before.astype(jnp.bfloat16), NN)
    code = jnp.where(named, rank, -1.0)
    gate = jnp.where(named, prob, 0.0)
    lines = [code[e : e + ROWS] for e in range(0, experts, ROWS)]
    others = [gate[e : e + ROWS] for e in range(0, experts, ROWS)]
    lines = [part for pair in zip(lines, others) for part in pair]
    blank = sent_ref.shape[1] - len(lines) * tokens
    if blank:
        lines.append(jnp.zeros((ROWS, blank), jnp.float32))
    sent_ref[tokens:] = jnp.concatenate(lines, axis=1).astype(jnp.bfloat16)


def expert_kernel(step, capacity, *refs):
    where_ref, gate_ref, up_ref, wg_ref, wu_ref, wd_ref = refs[:6]
    near_out, far_out, score_out = refs[-3:]
    token_refs = refs[6:-4]
    senders = score_out.shape[0]
    plane = senders // PLANES
    tok = token_refs[0].shape[0] - ROWS
    blocks = tok // BLK
    me = where_ref[0]
    low = me % plane
    group = jnp.bitwise_xor(me // plane, step)
    base = group * plane
    slots = plane * capacity
    stored = senders * capacity
    skew = (group * slots) % 8
    padded = -(-slots // 8) * 8
    start = pl.multiple_of(group * slots - skew, 8)
    score_out[...] = refs[-4][...]
    spots = [jnp.bitwise_xor(low, off) for off in range(plane)]
    own_row = lax.broadcasted_iota(jnp.int32, (ROWS, 2 * tok), 0) == me % ROWS
    lines = []
    for ref in token_refs:
        line = jnp.zeros((ROWS, 2 * tok), jnp.float32)
        for part in range(senders // ROWS):
            lanes = ref[tok:, 2 * part * tok : 2 * (part + 1) * tok].astype(jnp.float32)
            line = line + jnp.where(me // ROWS == part, lanes, 0.0)
        lines.append(jnp.sum(jnp.where(own_row, line, 0.0), axis=0, keepdims=True))
    number = lax.broadcasted_iota(jnp.int32, (padded, plane * BLK), 0).astype(jnp.float32)
    hits, places, rows, gates, firsts, seconds = [], [], [], [], [], []
    for b in range(blocks):
        keys, gate_row = [], []
        for spot, line in zip(spots, lines):
            code = line[:, b * BLK : (b + 1) * BLK]
            shift = (spot * capacity + skew).astype(jnp.float32)
            keys.append(jnp.where(code >= 0, code + shift, -1.0))
            gate_row.append(line[:, tok + b * BLK : tok + (b + 1) * BLK])
        hit = number == jnp.concatenate(keys, axis=1)
        place = hit.astype(jnp.float32).astype(jnp.bfloat16)
        tokens = jnp.concatenate([ref[b * BLK : (b + 1) * BLK] for ref in token_refs], axis=0)
        hits.append(hit)
        places.append(place)
        rows.append(dot(place, tokens, NN).astype(jnp.bfloat16))
        gate_row = jnp.concatenate(gate_row, axis=1)
        gates.append(jnp.sum(jnp.where(hit, gate_row, 0.0), axis=1, keepdims=True))
        window = pl.ds(b * stored + start, padded)
        firsts.append(gate_ref[window].astype(jnp.float32))
        seconds.append(up_ref[window].astype(jnp.float32))
    raw = dot(jnp.concatenate(rows, axis=0), wd_ref[...], NT)
    first = jnp.concatenate(firsts, axis=0)
    second = jnp.concatenate(seconds, axis=0)
    gate = jnp.concatenate(gates, axis=0)
    sigma = 1.0 / (1.0 + jnp.exp(-first))
    active = first * sigma
    slope = sigma * (1.0 + first * (1.0 - sigma))
    score = jnp.sum(raw * active * second, axis=1, keepdims=True)
    score = score.astype(jnp.bfloat16).astype(jnp.float32)
    scaled = gate * raw
    d_first = (scaled * second * slope).astype(jnp.bfloat16)
    d_second = (scaled * active).astype(jnp.bfloat16)
    back = dot(d_first, wg_ref[...], NN) + dot(d_second, wu_ref[...], NN)
    back = back.astype(jnp.bfloat16)
    scores = []
    for b in range(blocks):
        span = slice(b * padded, (b + 1) * padded)
        laid = dot(places[b], back[span], TN).astype(jnp.bfloat16)
        for off in range(plane):
            target = far_out if off % CORES else near_out
            target[off // CORES, b * BLK : (b + 1) * BLK] = laid[off * BLK : (off + 1) * BLK]
        scores.append(jnp.sum(jnp.where(hits[b], score[span], 0.0), axis=0, keepdims=True))
    for off, spot in enumerate(spots):
        span = slice(off * BLK, (off + 1) * BLK)
        score_out[base + spot] = jnp.concatenate([part[:, span] for part in scores], axis=1)


def expert_call(me, saved, weights, step, tokens, score, capacity):
    tok, width = tokens[0].shape
    laid = jax.ShapeDtypeStruct((len(tokens) // CORES, tok - ROWS, width), jnp.bfloat16)
    return call(
        functools.partial(expert_kernel, step, capacity),
        [laid, laid, jax.ShapeDtypeStruct(score.shape, score.dtype)],
        me, *saved, *weights, *tokens, score,
        spaces="s",
    )


def router_kernel(score_ref, prob_ref, hidden_ref, term_ref, logit_ref):
    prob = prob_ref[...]
    experts, _ = prob.shape
    score = score_ref[:, 0, :]
    logit = prob * (score - jnp.sum(prob * score, axis=0, keepdims=True))
    logit_ref[...] = logit
    term = sum(dot(part, hidden_ref[...], NN) for part in three_parts(logit))
    pieces, _, share = term_ref.shape
    for g in range(pieces // experts):
        term_ref[g * experts : (g + 1) * experts] = term[:, None, g * share : (g + 1) * share]


def share_kernel(piece_ref, share_ref, square_ref):
    total = jnp.sum(piece_ref[...], axis=0)
    share_ref[...] = total
    square = jnp.sum(total * total, axis=1, keepdims=True)
    square_ref[...] = jnp.broadcast_to(square, square_ref.shape)


def clip_kernel(entries, square_ref, share_ref, out_ref):
    total = jnp.sum(square_ref[...], axis=0)[:, :1]
    out_ref[...] = share_ref[...] * jnp.minimum(1.0, jnp.sqrt(entries / (total + 1e-06)))


def finish_kernel(*refs):
    logit_ref, router_ref, out_ref = refs[0], refs[1], refs[-1]
    total = lax.dot_general(
        logit_ref[...],
        router_ref[...],
        TN,
        precision=lax.Precision.HIGHEST,
        preferred_element_type=jnp.float32,
    )
    for ref in refs[2:-1]:
        total = total + ref[...].astype(jnp.float32)
    out_ref[...] = total.astype(out_ref.dtype)


def local(hidden, grad_out, router_weight, expert_ids, pre_gate, pre_up, w_gate, w_up, w_down):
    tokens, width = hidden.shape
    experts = router_weight.shape[1]
    blocks = tokens // BLK
    senders = lax.axis_size("expert")
    groups = lax.axis_size("dp")
    capacity = pre_gate.shape[2] // (blocks * senders)
    plane = senders // PLANES
    f32, bf16 = jnp.float32, jnp.bfloat16

    def swap(value, off):
        return lax.ppermute(value, "expert", [(i, i ^ off) for i in range(senders)])

    def exchange(value, axes):
        return lax.all_to_all(value, axes, 0, 0, tiled=True)

    router_rows = router_weight.T
    fronts = (hidden, router_rows, expert_ids.T, grad_out)
    sent, prob, me = call(
        front_kernel,
        [
            jax.ShapeDtypeStruct((tokens + ROWS, width), bf16),
            jax.ShapeDtypeStruct((experts, tokens), f32),
            jax.ShapeDtypeStruct((1,), jnp.int32),
        ],
        *fronts,
        lax.axis_index("expert").reshape(1),
        spaces="hhhhs",
        outs="vvs",
        scratch=[pltpu.VMEM(a.shape, a.dtype) for a in fronts[:3]]
        + [pltpu.SemaphoreType.DMA((4,))],
    )

    held = {0: sent}
    held[2 * plane] = swap(sent, 2 * plane)
    held[plane] = swap(sent, plane)
    held[3 * plane] = swap(held[2 * plane], plane)
    for k in range(PLANES):
        for y in range(CORES, plane, CORES):
            held[k * plane + y] = swap(held[k * plane], y)
    for off in range(0, senders, CORES):
        held[off + 1] = swap(held[off], 1)

    fetched = [a.reshape(a.shape[-2:]) for a in (pre_gate, pre_up)]
    fetched += [w_gate[0].T, w_up[0].T, w_down[0]]
    fetched = call(
        fetch_kernel,
        [jax.ShapeDtypeStruct(a.shape, a.dtype) for a in fetched],
        *fetched,
        spaces="hhhhh",
        scratch=[pltpu.SemaphoreType.DMA((len(fetched),))],
    )
    saved, weights = fetched[:2], fetched[2:]
    score = jnp.zeros((experts, 1, tokens), f32)
    totals = {}
    for k in (0, 2, 1, 3):
        pieces = [held[off] for off in range(k * plane, (k + 1) * plane)]
        near, far, score = expert_call(me, saved, weights, k, pieces, score, capacity)
        far = swap(far, 1)
        pair = [near[y].astype(f32) + far[y].astype(f32) for y in range(plane // CORES)]
        total = pair[0].astype(bf16).astype(f32)
        for y in range(1, plane // CORES):
            came = swap(pair[y].astype(bf16), y * CORES)
            total = total + came.astype(f32)
        totals[k] = total.astype(bf16)
    score = exchange(score, "expert")
    parts = [totals[0]] + [swap(totals[k], k * plane) for k in range(1, PLANES)]

    share = width // groups
    everyone = groups * senders
    term, logit = call(
        router_kernel,
        [
            jax.ShapeDtypeStruct((everyone, 1, share), f32),
            jax.ShapeDtypeStruct((experts, tokens), f32),
        ],
        score,
        prob,
        hidden,
        spaces="vvb",
    )
    pieces = exchange(term, ("dp", "expert"))
    column, square = call(
        share_kernel,
        [
            jax.ShapeDtypeStruct((1, share), f32),
            jax.ShapeDtypeStruct((everyone, 1, LANES), f32),
        ],
        pieces,
    )
    square = exchange(square, ("dp", "expert"))
    (update,) = call(
        functools.partial(clip_kernel, float(width * experts)),
        [jax.ShapeDtypeStruct((1, share), f32)],
        square,
        column,
    )
    (grad_x,) = call(
        finish_kernel,
        [jax.ShapeDtypeStruct((tokens, width), bf16)],
        logit,
        router_rows,
        *parts,
        spaces="vb",
    )
    return grad_x, update.reshape(share, 1)


def solution(mesh):
    placed = (
        P(("dp", "expert"), None),
        P(("dp", "expert"), None),
        P(),
        P(("dp", "expert"), None),
        P("dp", "expert", None, None),
        P("dp", "expert", None, None),
        P("expert", None, None),
        P("expert", None, None),
        P("expert", None, None),
    )
    return jax.shard_map(
        local,
        mesh=mesh,
        in_specs=placed,
        out_specs=(P(("dp", "expert"), None), P("dp", "expert")),
        check_vma=False,
    )
```

```python
import functools

import jax
import jax.numpy as jnp
from jax import lax
from jax.experimental import pallas as pl
from jax.experimental.pallas import tpu as pltpu
from jax.sharding import PartitionSpec as P


BLK = 64
LANES = 128
PLANES = 4
CORES = 2
ROWS = 8
ROOM = 6


NT = (((1,), (1,)), ((), ()))
TN = (((0,), (0,)), ((), ()))
NN = (((1,), (0,)), ((), ()))


def dot(left, right, dims):
    return lax.dot_general(left, right, dims, preferred_element_type=jnp.float32)


def three_parts(value):
    first = value.astype(jnp.bfloat16)
    rest = value - first.astype(jnp.float32)
    second = rest.astype(jnp.bfloat16)
    return first, second, (rest - second.astype(jnp.float32)).astype(jnp.bfloat16)


def call(kernel, out_shape, *operands, spaces="", outs="", scratch=()):
    kinds = {
        "v": pl.BlockSpec(memory_space=pltpu.VMEM),
        "b": pl.BlockSpec(),
        "s": pl.BlockSpec(memory_space=pltpu.SMEM),
        "h": pl.BlockSpec(memory_space=pltpu.HBM),
    }
    spaces = spaces.ljust(len(operands), "v")
    operands = [
        pltpu.with_memory_space_constraint(a, pltpu.HBM) if c == "h" else a
        for a, c in zip(operands, spaces)
    ]
    return pl.pallas_call(
        kernel,
        out_shape=out_shape,
        in_specs=[kinds[c] for c in spaces],
        out_specs=[kinds[c] for c in outs.ljust(len(out_shape), "v")],
        scratch_shapes=scratch,
        compiler_params=pltpu.CompilerParams(vmem_limit_bytes=ROOM << 20),
    )(*operands)


def fetch_kernel(*refs):
    count = (len(refs) - 1) // 2
    copies = [
        pltpu.make_async_copy(refs[i], refs[count + i], refs[-1].at[i]) for i in range(count)
    ]
    for copy in copies:
        copy.start()
    for copy in copies:
        copy.wait()


def front_kernel(*refs):
    sent_ref, prob_ref, me_ref, hidden_ref, router_ref, ids_ref, sems = refs[5:]
    me_ref[0] = refs[4][0]
    experts, tokens = prob_ref.shape
    targets = (hidden_ref, router_ref, ids_ref, sent_ref.at[pl.ds(0, tokens)])
    copies = [pltpu.make_async_copy(refs[i], targets[i], sems.at[i]) for i in range(4)]
    for copy in copies:
        copy.start()
    for copy in copies:
        copy.wait()
    hidden = hidden_ref[...]
    logits = sum(dot(part, hidden, NT) for part in three_parts(router_ref[...]))
    exponent = jnp.exp(logits)
    prob = exponent / jnp.sum(exponent, axis=0, keepdims=True)
    prob_ref[...] = prob
    number = lax.broadcasted_iota(jnp.int32, (experts, tokens), 0)
    ids = ids_ref[...]
    named = number == ids[0:1, :]
    for k in range(1, ids.shape[0]):
        named = named | (number == ids[k : k + 1, :])
    row = lax.broadcasted_iota(jnp.int32, (tokens, tokens), 0)
    column = lax.broadcasted_iota(jnp.int32, (tokens, tokens), 1)
    before = (row < column) & (row // BLK == column // BLK)
    rank = dot(named.astype(jnp.bfloat16), before.astype(jnp.bfloat16), NN)
    code = jnp.where(named, rank, -1.0)
    gate = jnp.where(named, prob, 0.0)
    lines = [code[e : e + ROWS] for e in range(0, experts, ROWS)]
    others = [gate[e : e + ROWS] for e in range(0, experts, ROWS)]
    lines = [part for pair in zip(lines, others) for part in pair]
    blank = sent_ref.shape[1] - len(lines) * tokens
    if blank:
        lines.append(jnp.zeros((ROWS, blank), jnp.float32))
    sent_ref[tokens:] = jnp.concatenate(lines, axis=1).astype(jnp.bfloat16)


def expert_kernel(step, capacity, plane, extra, *refs):
    where_ref, gate_ref, up_ref, wg_ref, wu_ref, wd_ref = refs[:6]
    token_refs, refs = refs[6 : 6 + plane], refs[6 + plane :]
    (score_ref, *carried), refs = refs[: 1 + extra], refs[1 + extra :]
    near_out, far_out, score_out, *pair_outs = refs
    for y in range(plane // CORES if extra else 0):
        both = carried[0][y].astype(jnp.float32) + carried[1][y].astype(jnp.float32)
        pair_outs[y][...] = both.astype(jnp.bfloat16)
    senders = score_out.shape[0]
    tok = token_refs[0].shape[0] - ROWS
    blocks = tok // BLK
    me = where_ref[0]
    low = me % plane
    group = jnp.bitwise_xor(me // plane, step)
    base = group * plane
    slots = plane * capacity
    stored = senders * capacity
    skew = (group * slots) % 8
    padded = -(-slots // 8) * 8
    start = pl.multiple_of(group * slots - skew, 8)
    score_out[...] = score_ref[...]
    spots = [jnp.bitwise_xor(low, off) for off in range(plane)]
    own_row = lax.broadcasted_iota(jnp.int32, (ROWS, 2 * tok), 0) == me % ROWS
    lines = []
    for ref in token_refs:
        line = jnp.zeros((ROWS, 2 * tok), jnp.float32)
        for part in range(senders // ROWS):
            lanes = ref[tok:, 2 * part * tok : 2 * (part + 1) * tok].astype(jnp.float32)
            line = line + jnp.where(me // ROWS == part, lanes, 0.0)
        lines.append(jnp.sum(jnp.where(own_row, line, 0.0), axis=0, keepdims=True))
    number = lax.broadcasted_iota(jnp.int32, (padded, plane * BLK), 0).astype(jnp.float32)
    hits, places, rows, gates, firsts, seconds = [], [], [], [], [], []
    for b in range(blocks):
        keys, gate_row = [], []
        for spot, line in zip(spots, lines):
            code = line[:, b * BLK : (b + 1) * BLK]
            shift = (spot * capacity + skew).astype(jnp.float32)
            keys.append(jnp.where(code >= 0, code + shift, -1.0))
            gate_row.append(line[:, tok + b * BLK : tok + (b + 1) * BLK])
        hit = number == jnp.concatenate(keys, axis=1)
        place = hit.astype(jnp.float32).astype(jnp.bfloat16)
        tokens = jnp.concatenate([ref[b * BLK : (b + 1) * BLK] for ref in token_refs], axis=0)
        hits.append(hit)
        places.append(place)
        rows.append(dot(place, tokens, NN).astype(jnp.bfloat16))
        gate_row = jnp.concatenate(gate_row, axis=1)
        gates.append(jnp.sum(jnp.where(hit, gate_row, 0.0), axis=1, keepdims=True))
        window = pl.ds(b * stored + start, padded)
        firsts.append(gate_ref[window])
        seconds.append(up_ref[window])
    rows = jnp.concatenate(rows, axis=0)
    gate = jnp.concatenate(gates, axis=0)
    hidden_units = wd_ref.shape[0]
    cuts = [0, -(-hidden_units // 2 // LANES) * LANES, hidden_units]
    score, down_first, down_second = 0.0, [], []
    for lo, hi in zip(cuts, cuts[1:]):
        raw = dot(rows, wd_ref[lo:hi], NT)
        first = jnp.concatenate([part[:, lo:hi] for part in firsts], axis=0).astype(jnp.float32)
        second = jnp.concatenate([part[:, lo:hi] for part in seconds], axis=0).astype(jnp.float32)
        sigma = 1.0 / (1.0 + jnp.exp(-first))
        active = first * sigma
        slope = sigma * (1.0 + first * (1.0 - sigma))
        score = score + jnp.sum(raw * active * second, axis=1, keepdims=True)
        scaled = gate * raw
        down_first.append((scaled * second * slope).astype(jnp.bfloat16))
        down_second.append((scaled * active).astype(jnp.bfloat16))
    score = score.astype(jnp.bfloat16).astype(jnp.float32)
    stacked = jnp.concatenate([wg_ref[...], wu_ref[...]], axis=0)
    back = dot(jnp.concatenate(down_first + down_second, axis=1), stacked, NN)
    back = back.astype(jnp.bfloat16)
    for b in range(blocks):
        laid = dot(places[b], back[b * padded : (b + 1) * padded], TN).astype(jnp.bfloat16)
        for off in range(plane):
            target = far_out if off % CORES else near_out
            target[off // CORES, b * BLK : (b + 1) * BLK] = laid[off * BLK : (off + 1) * BLK]
    scores = []
    for b in range(blocks):
        span = slice(b * padded, (b + 1) * padded)
        scores.append(jnp.sum(jnp.where(hits[b], score[span], 0.0), axis=0, keepdims=True))
    for off, spot in enumerate(spots):
        span = slice(off * BLK, (off + 1) * BLK)
        score_out[base + spot] = jnp.concatenate([part[:, span] for part in scores], axis=1)


def expert_call(me, saved, weights, step, tokens, score, carried, capacity):
    tok, width = tokens[0].shape
    sums = len(tokens) // CORES
    laid = jax.ShapeDtypeStruct((sums, tok - ROWS, width), jnp.bfloat16)
    pair = [jax.ShapeDtypeStruct(laid.shape[1:], laid.dtype)] * sums
    return call(
        functools.partial(expert_kernel, step, capacity, len(tokens), len(carried)),
        [laid, laid, jax.ShapeDtypeStruct(score.shape, score.dtype)] + (pair if carried else []),
        me, *saved, *weights, *tokens, score, *carried,
        spaces="s",
    )


def router_kernel(score_ref, prob_ref, hidden_ref, term_ref, logit_ref):
    prob = prob_ref[...]
    experts, _ = prob.shape
    score = score_ref[:, 0, :]
    logit = prob * (score - jnp.sum(prob * score, axis=0, keepdims=True))
    logit_ref[...] = logit
    term = sum(dot(part, hidden_ref[...], NN) for part in three_parts(logit))
    pieces, _, share = term_ref.shape
    for g in range(pieces // experts):
        term_ref[g * experts : (g + 1) * experts] = term[:, None, g * share : (g + 1) * share]


def share_kernel(piece_ref, share_ref, square_ref):
    total = jnp.sum(piece_ref[...], axis=0)
    share_ref[...] = total
    square = jnp.sum(total * total, axis=1, keepdims=True)
    square_ref[...] = jnp.broadcast_to(square, square_ref.shape)


def clip_kernel(entries, square_ref, share_ref, out_ref):
    total = jnp.sum(square_ref[...], axis=0)[:, :1]
    out_ref[...] = share_ref[...] * jnp.minimum(1.0, jnp.sqrt(entries / (total + 1e-06)))


def finish_kernel(*refs):
    logit_ref, router_ref, out_ref = refs[0], refs[1], refs[-1]
    l0, l1, l2 = three_parts(logit_ref[...])
    r0, r1, r2 = three_parts(router_ref[...])
    left = jnp.concatenate([l0, l0, l1, l0, l1, l2], axis=0)
    right = jnp.concatenate([r0, r1, r0, r2, r1, r0], axis=0)
    total = dot(left, right, TN)
    for ref in refs[2:-1]:
        total = total + ref[...].astype(jnp.float32)
    out_ref[...] = total.astype(out_ref.dtype)


def local(hidden, grad_out, router_weight, expert_ids, pre_gate, pre_up, w_gate, w_up, w_down):
    tokens, width = hidden.shape
    experts = router_weight.shape[1]
    blocks = tokens // BLK
    senders = lax.axis_size("expert")
    groups = lax.axis_size("dp")
    capacity = pre_gate.shape[2] // (blocks * senders)
    plane = senders // PLANES
    f32, bf16 = jnp.float32, jnp.bfloat16

    def swap(value, off):
        return lax.ppermute(value, "expert", [(i, i ^ off) for i in range(senders)])

    def exchange(value, axes):
        return lax.all_to_all(value, axes, 0, 0, tiled=True)

    router_rows = router_weight.T
    fronts = (hidden, router_rows, expert_ids.T, grad_out)
    sent, prob, me = call(
        front_kernel,
        [
            jax.ShapeDtypeStruct((tokens + ROWS, width), bf16),
            jax.ShapeDtypeStruct((experts, tokens), f32),
            jax.ShapeDtypeStruct((1,), jnp.int32),
        ],
        *fronts,
        lax.axis_index("expert").reshape(1),
        spaces="hhhhs",
        outs="vvs",
        scratch=[pltpu.VMEM(a.shape, a.dtype) for a in fronts[:3]]
        + [pltpu.SemaphoreType.DMA((4,))],
    )

    held = {0: sent}
    held[2 * plane] = swap(sent, 2 * plane)
    held[plane] = swap(sent, plane)
    held[3 * plane] = swap(held[2 * plane], plane)
    for y in range(CORES, plane, CORES):
        for k in (0, 2, 3):
            held[k * plane + y] = swap(held[k * plane], y)
        held[plane + y] = swap(held[y], plane)
    for off in range(0, senders, CORES):
        held[off + 1] = swap(held[off], 1)

    fetched = [a.reshape(a.shape[-2:]) for a in (pre_gate, pre_up)]
    fetched += [w_gate[0].T, w_up[0].T, w_down[0]]
    fetched = call(
        fetch_kernel,
        [jax.ShapeDtypeStruct(a.shape, a.dtype) for a in fetched],
        *fetched,
        spaces="hhhhh",
        scratch=[pltpu.SemaphoreType.DMA((len(fetched),))],
    )
    saved, weights = fetched[:2], fetched[2:]
    score = jnp.zeros((experts, 1, tokens), f32)
    carried, before, pairs = (), None, {}
    for k in (0, 2, 1, 3):
        pieces = [held[off] for off in range(k * plane, (k + 1) * plane)]
        near, far, score, *pair = expert_call(
            me, saved, weights, k, pieces, score, carried, capacity
        )
        if pair:
            pairs[before] = pair
        carried, before = (near, swap(far, 1)), k
    near, far = carried
    pairs[before] = [
        (near[y].astype(f32) + far[y].astype(f32)).astype(bf16) for y in range(plane // CORES)
    ]
    score = exchange(score, "expert")

    def along_y(pair):
        came = [swap(pair[y], y * CORES) for y in range(1, plane // CORES)]
        return sum(part.astype(f32) for part in [pair[0], *came]).astype(bf16)

    parts = [pairs[0][0]]
    parts += [swap(pairs[0][y], y * CORES) for y in range(1, plane // CORES)]
    parts += [swap(along_y(pairs[k]), k * plane) for k in range(1, PLANES)]

    share = width // groups
    everyone = groups * senders
    term, logit = call(
        router_kernel,
        [
            jax.ShapeDtypeStruct((everyone, 1, share), f32),
            jax.ShapeDtypeStruct((experts, tokens), f32),
        ],
        score,
        prob,
        hidden,
        spaces="vvb",
    )
    pieces = exchange(term, ("dp", "expert"))
    column, square = call(
        share_kernel,
        [
            jax.ShapeDtypeStruct((1, share), f32),
            jax.ShapeDtypeStruct((everyone, 1, LANES), f32),
        ],
        pieces,
    )
    square = exchange(square, ("dp", "expert"))
    (update,) = call(
        functools.partial(clip_kernel, float(width * experts)),
        [jax.ShapeDtypeStruct((1, share), f32)],
        square,
        column,
    )
    (grad_x,) = call(
        finish_kernel,
        [jax.ShapeDtypeStruct((tokens, width), bf16)],
        logit,
        router_rows,
        *parts,
        spaces="vb",
    )
    return grad_x, update.reshape(share, 1)


def solution(mesh):
    placed = (
        P(("dp", "expert"), None),
        P(("dp", "expert"), None),
        P(),
        P(("dp", "expert"), None),
        P("dp", "expert", None, None),
        P("dp", "expert", None, None),
        P("expert", None, None),
        P("expert", None, None),
        P("expert", None, None),
    )
    return jax.shard_map(
        local,
        mesh=mesh,
        in_specs=placed,
        out_specs=(P(("dp", "expert"), None), P("dp", "expert")),
        check_vma=False,
    )
```

```python
import functools

import jax
import jax.numpy as jnp
from jax import lax
from jax.experimental import pallas as pl
from jax.experimental.pallas import tpu as pltpu
from jax.sharding import PartitionSpec as P


BLK = 64
LANES = 128
PLANES = 4
CORES = 2
ROWS = 8
ROOM = 6


NT = (((1,), (1,)), ((), ()))
TN = (((0,), (0,)), ((), ()))
NN = (((1,), (0,)), ((), ()))


def dot(left, right, dims):
    return lax.dot_general(left, right, dims, preferred_element_type=jnp.float32)


def three_parts(value):
    first = value.astype(jnp.bfloat16)
    rest = value - first.astype(jnp.float32)
    second = rest.astype(jnp.bfloat16)
    return first, second, (rest - second.astype(jnp.float32)).astype(jnp.bfloat16)


def call(kernel, out_shape, *operands, spaces="", outs="", scratch=()):
    kinds = {
        "v": pl.BlockSpec(memory_space=pltpu.VMEM),
        "b": pl.BlockSpec(),
        "s": pl.BlockSpec(memory_space=pltpu.SMEM),
        "h": pl.BlockSpec(memory_space=pltpu.HBM),
    }
    spaces = spaces.ljust(len(operands), "v")
    operands = [
        pltpu.with_memory_space_constraint(a, pltpu.HBM) if c == "h" else a
        for a, c in zip(operands, spaces)
    ]
    return pl.pallas_call(
        kernel,
        out_shape=out_shape,
        in_specs=[kinds[c] for c in spaces],
        out_specs=[kinds[c] for c in outs.ljust(len(out_shape), "v")],
        scratch_shapes=scratch,
        compiler_params=pltpu.CompilerParams(vmem_limit_bytes=ROOM << 20),
    )(*operands)


def fetch_kernel(*refs):
    count = (len(refs) - 1) // 2
    copies = [
        pltpu.make_async_copy(refs[i], refs[count + i], refs[-1].at[i]) for i in range(count)
    ]
    for copy in copies:
        copy.start()
    for copy in copies:
        copy.wait()


def front_kernel(*refs):
    sent_ref, prob_ref, me_ref, hidden_ref, router_ref, ids_ref, sems = refs[5:]
    me_ref[0] = refs[4][0]
    experts, tokens = prob_ref.shape
    targets = (hidden_ref, router_ref, ids_ref, sent_ref.at[pl.ds(0, tokens)])
    copies = [pltpu.make_async_copy(refs[i], targets[i], sems.at[i]) for i in range(4)]
    for copy in copies:
        copy.start()
    for copy in copies:
        copy.wait()
    hidden = hidden_ref[...]
    logits = sum(dot(part, hidden, NT) for part in three_parts(router_ref[...]))
    exponent = jnp.exp(logits)
    prob = exponent / jnp.sum(exponent, axis=0, keepdims=True)
    prob_ref[...] = prob
    number = lax.broadcasted_iota(jnp.int32, (experts, tokens), 0)
    ids = ids_ref[...]
    named = number == ids[0:1, :]
    for k in range(1, ids.shape[0]):
        named = named | (number == ids[k : k + 1, :])
    row = lax.broadcasted_iota(jnp.int32, (tokens, tokens), 0)
    column = lax.broadcasted_iota(jnp.int32, (tokens, tokens), 1)
    before = (row < column) & (row // BLK == column // BLK)
    rank = dot(named.astype(jnp.bfloat16), before.astype(jnp.bfloat16), NN)
    code = jnp.where(named, rank, -1.0)
    gate = jnp.where(named, prob, 0.0)
    lines = [code[e : e + ROWS] for e in range(0, experts, ROWS)]
    others = [gate[e : e + ROWS] for e in range(0, experts, ROWS)]
    lines = [part for pair in zip(lines, others) for part in pair]
    blank = sent_ref.shape[1] - len(lines) * tokens
    if blank:
        lines.append(jnp.zeros((ROWS, blank), jnp.float32))
    sent_ref[tokens:] = jnp.concatenate(lines, axis=1).astype(jnp.bfloat16)


def expert_kernel(step, capacity, plane, extra, *refs):
    where_ref, gate_ref, up_ref, wg_ref, wu_ref, wd_ref = refs[:6]
    token_refs, refs = refs[6 : 6 + plane], refs[6 + plane :]
    (score_ref, *carried), refs = refs[: 1 + extra], refs[1 + extra :]
    near_out, far_out, score_out, *pair_outs = refs
    for y in range(plane // CORES if extra else 0):
        both = carried[0][y].astype(jnp.float32) + carried[1][y].astype(jnp.float32)
        pair_outs[y][...] = both.astype(jnp.bfloat16)
    senders = score_out.shape[0]
    tok = token_refs[0].shape[0] - ROWS
    blocks = tok // BLK
    me = where_ref[0]
    low = me % plane
    group = jnp.bitwise_xor(me // plane, step)
    base = group * plane
    slots = plane * capacity
    stored = senders * capacity
    skew = (group * slots) % 8
    padded = -(-slots // 8) * 8
    start = pl.multiple_of(group * slots - skew, 8)
    score_out[...] = score_ref[...]
    spots = [jnp.bitwise_xor(low, off) for off in range(plane)]
    own_row = lax.broadcasted_iota(jnp.int32, (ROWS, 2 * tok), 0) == me % ROWS
    lines = []
    for ref in token_refs:
        line = jnp.zeros((ROWS, 2 * tok), jnp.float32)
        for part in range(senders // ROWS):
            lanes = ref[tok:, 2 * part * tok : 2 * (part + 1) * tok].astype(jnp.float32)
            line = line + jnp.where(me // ROWS == part, lanes, 0.0)
        lines.append(jnp.sum(jnp.where(own_row, line, 0.0), axis=0, keepdims=True))
    number = lax.broadcasted_iota(jnp.int32, (padded, plane * BLK), 0).astype(jnp.float32)
    hits, places, rows, gates, firsts, seconds = [], [], [], [], [], []
    for b in range(blocks):
        keys, gate_row = [], []
        for spot, line in zip(spots, lines):
            code = line[:, b * BLK : (b + 1) * BLK]
            shift = (spot * capacity + skew).astype(jnp.float32)
            keys.append(jnp.where(code >= 0, code + shift, -1.0))
            gate_row.append(line[:, tok + b * BLK : tok + (b + 1) * BLK])
        hit = number == jnp.concatenate(keys, axis=1)
        place = hit.astype(jnp.float32).astype(jnp.bfloat16)
        tokens = jnp.concatenate([ref[b * BLK : (b + 1) * BLK] for ref in token_refs], axis=0)
        hits.append(hit)
        places.append(place)
        rows.append(dot(place, tokens, NN).astype(jnp.bfloat16))
        gate_row = jnp.concatenate(gate_row, axis=1)
        gates.append(jnp.sum(jnp.where(hit, gate_row, 0.0), axis=1, keepdims=True))
        window = pl.ds(b * stored + start, padded)
        firsts.append(gate_ref[window])
        seconds.append(up_ref[window])
    rows = jnp.concatenate(rows, axis=0)
    gate = jnp.concatenate(gates, axis=0)
    hidden_units = wd_ref.shape[0]
    cuts = [0, -(-hidden_units // 2 // LANES) * LANES, hidden_units]
    score, down_first, down_second = 0.0, [], []
    for lo, hi in zip(cuts, cuts[1:]):
        raw = dot(rows, wd_ref[lo:hi], NT)
        first = jnp.concatenate([part[:, lo:hi] for part in firsts], axis=0).astype(jnp.float32)
        second = jnp.concatenate([part[:, lo:hi] for part in seconds], axis=0).astype(jnp.float32)
        sigma = 1.0 / (1.0 + jnp.exp(-first))
        active = first * sigma
        slope = sigma * (1.0 + first * (1.0 - sigma))
        score = score + jnp.sum(raw * active * second, axis=1, keepdims=True)
        scaled = gate * raw
        down_first.append((scaled * second * slope).astype(jnp.bfloat16))
        down_second.append((scaled * active).astype(jnp.bfloat16))
    score = score.astype(jnp.bfloat16).astype(jnp.float32)
    stacked = jnp.concatenate([wg_ref[...], wu_ref[...]], axis=0)
    back = dot(jnp.concatenate(down_first + down_second, axis=1), stacked, NN)
    back = back.astype(jnp.bfloat16)
    for b in range(blocks):
        laid = dot(places[b], back[b * padded : (b + 1) * padded], TN).astype(jnp.bfloat16)
        for off in range(plane):
            target = far_out if off % CORES else near_out
            target[off // CORES, b * BLK : (b + 1) * BLK] = laid[off * BLK : (off + 1) * BLK]
    scores = []
    for b in range(blocks):
        span = slice(b * padded, (b + 1) * padded)
        scores.append(jnp.sum(jnp.where(hits[b], score[span], 0.0), axis=0, keepdims=True))
    for off, spot in enumerate(spots):
        span = slice(off * BLK, (off + 1) * BLK)
        score_out[base + spot] = jnp.concatenate([part[:, span] for part in scores], axis=1)


def expert_call(me, saved, weights, step, tokens, score, carried, capacity):
    tok, width = tokens[0].shape
    sums = len(tokens) // CORES
    laid = jax.ShapeDtypeStruct((sums, tok - ROWS, width), jnp.bfloat16)
    pair = [jax.ShapeDtypeStruct(laid.shape[1:], laid.dtype)] * sums
    return call(
        functools.partial(expert_kernel, step, capacity, len(tokens), len(carried)),
        [laid, laid, jax.ShapeDtypeStruct(score.shape, score.dtype)] + (pair if carried else []),
        me, *saved, *weights, *tokens, score, *carried,
        spaces="s",
    )


def router_kernel(score_ref, prob_ref, hidden_ref, term_ref, logit_ref):
    prob = prob_ref[...]
    experts, _ = prob.shape
    score = score_ref[:, 0, :]
    logit = prob * (score - jnp.sum(prob * score, axis=0, keepdims=True))
    logit_ref[...] = logit
    term = sum(dot(part, hidden_ref[...], NN) for part in three_parts(logit))
    pieces, _, share = term_ref.shape
    for g in range(pieces // experts):
        term_ref[g * experts : (g + 1) * experts] = term[:, None, g * share : (g + 1) * share]


def share_kernel(piece_ref, share_ref, square_ref):
    total = jnp.sum(piece_ref[...], axis=0)
    share_ref[...] = total
    square = jnp.sum(total * total, axis=1, keepdims=True)
    square_ref[...] = jnp.broadcast_to(square, square_ref.shape)


def clip_kernel(entries, square_ref, share_ref, out_ref):
    total = jnp.sum(square_ref[...], axis=0)[:, :1]
    out_ref[...] = share_ref[...] * jnp.minimum(1.0, jnp.sqrt(entries / (total + 1e-06)))


def finish_kernel(*refs):
    logit_ref, router_ref, out_ref = refs[0], refs[1], refs[-1]
    l0, l1, l2 = three_parts(logit_ref[...])
    r0, r1, r2 = three_parts(router_ref[...])
    left = jnp.concatenate([l0, l0, l1, l0, l1, l2], axis=0)
    right = jnp.concatenate([r0, r1, r0, r2, r1, r0], axis=0)
    total = dot(left, right, TN)
    for ref in refs[2:-1]:
        total = total + ref[...].astype(jnp.float32)
    out_ref[...] = total.astype(out_ref.dtype)


def local(hidden, grad_out, router_weight, expert_ids, pre_gate, pre_up, w_gate, w_up, w_down):
    tokens, width = hidden.shape
    experts = router_weight.shape[1]
    blocks = tokens // BLK
    senders = lax.axis_size("expert")
    groups = lax.axis_size("dp")
    capacity = pre_gate.shape[2] // (blocks * senders)
    plane = senders // PLANES
    f32, bf16 = jnp.float32, jnp.bfloat16

    def swap(value, off):
        return lax.ppermute(value, "expert", [(i, i ^ off) for i in range(senders)])

    def exchange(value, axes):
        return lax.all_to_all(value, axes, 0, 0, tiled=True)

    router_rows = router_weight.T
    fronts = (hidden, router_rows, expert_ids.T, grad_out)
    sent, prob, me = call(
        front_kernel,
        [
            jax.ShapeDtypeStruct((tokens + ROWS, width), bf16),
            jax.ShapeDtypeStruct((experts, tokens), f32),
            jax.ShapeDtypeStruct((1,), jnp.int32),
        ],
        *fronts,
        lax.axis_index("expert").reshape(1),
        spaces="hhhhs",
        outs="vvs",
        scratch=[pltpu.VMEM(a.shape, a.dtype) for a in fronts[:3]]
        + [pltpu.SemaphoreType.DMA((4,))],
    )

    held = {0: sent}
    held[2 * plane] = swap(sent, 2 * plane)
    held[plane] = swap(sent, plane)
    held[3 * plane] = swap(held[2 * plane], plane)
    for y in range(CORES, plane, CORES):
        for k in (0, 2, 3):
            held[k * plane + y] = swap(held[k * plane], y)
        held[plane + y] = swap(held[y], plane)
    for off in range(0, senders, CORES):
        held[off + 1] = swap(held[off], 1)

    fetched = [a.reshape(a.shape[-2:]) for a in (pre_gate, pre_up)]
    fetched += [w_gate[0].T, w_up[0].T, w_down[0]]
    fetched = call(
        fetch_kernel,
        [jax.ShapeDtypeStruct(a.shape, a.dtype) for a in fetched],
        *fetched,
        spaces="hhhhh",
        scratch=[pltpu.SemaphoreType.DMA((len(fetched),))],
    )
    saved, weights = fetched[:2], fetched[2:]
    score = jnp.zeros((experts, 1, tokens), f32)
    carried, before, pairs = (), None, {}
    for k in (0, 2, 1, 3):
        pieces = [held[off] for off in range(k * plane, (k + 1) * plane)]
        near, far, score, *pair = expert_call(
            me, saved, weights, k, pieces, score, carried, capacity
        )
        if pair:
            pairs[before] = pair
        far = swap(far, 1)
        carried, before = (near, far), k
        if k == 0:
            pairs[0] = [
                (near[y].astype(f32) + far[y].astype(f32)).astype(bf16)
                for y in range(plane // CORES)
            ]
            carried = ()
    near, far = carried
    pairs[before] = [
        (near[y].astype(f32) + far[y].astype(f32)).astype(bf16) for y in range(plane // CORES)
    ]
    score = exchange(score, "expert")

    def along_y(pair):
        came = [swap(pair[y], y * CORES) for y in range(1, plane // CORES)]
        return sum(part.astype(f32) for part in [pair[0], *came]).astype(bf16)

    parts = [pairs[0][0]]
    parts += [swap(pairs[0][y], y * CORES) for y in range(1, plane // CORES)]
    parts += [swap(along_y(pairs[k]), k * plane) for k in range(1, PLANES)]

    share = width // groups
    everyone = groups * senders
    term, logit = call(
        router_kernel,
        [
            jax.ShapeDtypeStruct((everyone, 1, share), f32),
            jax.ShapeDtypeStruct((experts, tokens), f32),
        ],
        score,
        prob,
        hidden,
        spaces="vvb",
    )
    pieces = exchange(term, ("dp", "expert"))
    column, square = call(
        share_kernel,
        [
            jax.ShapeDtypeStruct((1, share), f32),
            jax.ShapeDtypeStruct((everyone, 1, LANES), f32),
        ],
        pieces,
    )
    square = exchange(square, ("dp", "expert"))
    (update,) = call(
        functools.partial(clip_kernel, float(width * experts)),
        [jax.ShapeDtypeStruct((1, share), f32)],
        square,
        column,
    )
    (grad_x,) = call(
        finish_kernel,
        [jax.ShapeDtypeStruct((tokens, width), bf16)],
        logit,
        router_rows,
        *parts,
        spaces="vb",
    )
    return grad_x, update.reshape(share, 1)


def solution(mesh):
    placed = (
        P(("dp", "expert"), None),
        P(("dp", "expert"), None),
        P(),
        P(("dp", "expert"), None),
        P("dp", "expert", None, None),
        P("dp", "expert", None, None),
        P("expert", None, None),
        P("expert", None, None),
        P("expert", None, None),
    )
    return jax.shard_map(
        local,
        mesh=mesh,
        in_specs=placed,
        out_specs=(P(("dp", "expert"), None), P("dp", "expert")),
        check_vma=False,
    )
```
